32 devices in a mesh: tp: 2 (over x), ctx: 4 (over y, core), rep: 4 (over z).
Axes of the slice: x: 2, y: 2, z: 4, core: 2. Of those that a mesh axis runs over, the one named last changes fastest.
Arguments:
- tokens: bfloat16 [4, 4, 336, 2048], P('rep', 'ctx', 'tp'), may hold values from -6 to 6
- cotangent: bfloat16 [4, 4, 336, 2048], P('rep', 'ctx', 'tp'), may hold values from -6 to 6
- positions: int32 [4, 1344], P('rep', 'ctx'), may hold values from 0 to 647, as said below
- seg_start: int32 [4, 13], P('rep'), may hold values from 0 to 1272, as said below
- seg_parent: int32 [4, 13], P('rep'), may hold values from 0 to 4, as said below
- ln_gain: bfloat16 [2048], replicated, may hold values from 0.5 to 1.5
- ln_bias: bfloat16 [2048], replicated, may hold values from -1.25 to 1.25
- w_qkv: bfloat16 [2048, 3, 2048], P(None, None, 'tp'), may hold values from -0.125 to 0.125
- b_qkv: bfloat16 [3, 2048], P(None, 'tp'), may hold values from -0.3125 to 0.3125
- w_dense: bfloat16 [2048, 2048], P('tp'), may hold values from -2 to 2
- b_dense: bfloat16 [2048], replicated, may hold values from -1.25 to 1.25
- w_fc1: bfloat16 [2048, 8192], P(None, 'tp'), may hold values from -0.125 to 0.125
- b_fc1: bfloat16 [8192], P('tp'), may hold values from -3 to 3
- w_fc2: bfloat16 [8192, 2048], P('tp'), may hold values from -0.0625 to 0.0625
- b_fc2: bfloat16 [2048], replicated, may hold values from -1.25 to 1.25
Outputs:
- block_out: bfloat16 [4, 4, 336, 2048], P('rep', 'ctx', 'tp')
- d_tokens: float32 [4, 4, 336, 2048], P('rep', 'ctx', 'tp')
- g_ln_gain: float32 [2048], P(('tp', 'ctx', 'rep'))
- g_ln_bias: float32 [2048], P(('tp', 'ctx', 'rep'))
- g_qkv: float32 [2048, 3, 2048], P(('ctx', 'rep'), None, 'tp')
- g_qkv_bias: float32 [3, 2048], P(None, ('tp', 'ctx', 'rep'))
- g_dense: float32 [2048, 2048], P(('tp', 'ctx', 'rep'))
- g_dense_bias: float32 [2048], P(('tp', 'ctx', 'rep'))
- g_fc1: float32 [2048, 8192], P(('ctx', 'rep'), 'tp')
- g_fc1_bias: float32 [8192], P(('tp', 'ctx', 'rep'))
- g_fc2: float32 [8192, 2048], P(('tp', 'ctx', 'rep'))
- g_fc2_bias: float32 [2048], P(('tp', 'ctx', 'rep'))
The draws below stay inside these ranges and needn't reach their ends.
Inputs may be any that keep to these rules, and one draw needn't show every extreme that they name: Each tree is packed as its trunk (segment 0), then its four branches (segments 1 to 4), then its eight leaves (segments 5 to 12); seg_start rises and its first entry is 0; every segment holds at least one token; seg_start[s + 1] - seg_start[s] and 1344 - seg_start[12] are the lengths. `seg_parent`: the trunk and the branches name 0; each leaf names a branch, and every branch has exactly two leaves. `positions`: A token's offset in its segment plus the lengths of its ancestor segments.
All inputs are finite; a program needn't handle non-finite values.
Results may differ from the reference program's by a relative error of at most 0.014.
Values may be sent and summed in bfloat16 or wider, within the bound.
A program may use at most 320 MiB of HBM per device.

```python
import math
import jax
import jax.numpy as jnp
from jax import lax

D = 2048
HEADS = 32
HEAD = 64
ROT = 32
FF = 8192
TOK_CTX = 336
SEGS = 13
TREE = 1344
TREES = 4
N_CTX = 4


def tree_layout(key):
    unit_len = TREE // 28
    half_unit = TREE // 56

    def one_tree(tree_key):
        shift_key, sway_key, leaf_key = jax.random.split(tree_key, 3)
        free_shifts = jax.random.randint(shift_key, (2,), -half_unit, 1)
        third_shift = -unit_len - jnp.sum(free_shifts)
        shifts = jnp.concatenate([free_shifts, third_shift[None], jnp.full((1,), unit_len, jnp.int32)]).astype(jnp.int32)
        drawn_sways = jax.random.randint(sway_key, (4,), -half_unit, half_unit + 1)
        leaf_sways = jnp.where(jnp.arange(4, dtype=jnp.int32) == 3, -half_unit, drawn_sways)
        first_parents = jax.random.permutation(leaf_key, jnp.array([1, 1, 2, 2, 3, 3, 4], dtype=jnp.int32))
        leaf_parents = jnp.concatenate([first_parents, jnp.full((1,), 4, jnp.int32)])
        trunk_length = 8 * unit_len - jnp.sum(shifts)
        branches = 3 * unit_len + shifts
        leaves = jnp.stack([unit_len + leaf_sways, unit_len - leaf_sways], axis=1).reshape(8)
        lengths = jnp.concatenate([trunk_length[None], branches, leaves]).astype(jnp.int32)
        starts = (jnp.cumsum(lengths) - lengths).astype(jnp.int32)
        parents = jnp.concatenate([jnp.zeros((5,), jnp.int32), leaf_parents.astype(jnp.int32)])
        token_index = jnp.arange(TREE, dtype=jnp.int32)
        segment = jnp.sum((starts[None, :] <= token_index[:, None]).astype(jnp.int32), axis=1) - 1
        seg_ids = jnp.arange(SEGS, dtype=jnp.int32)
        onehot = segment[:, None] == seg_ids[None, :]
        own_start = jnp.sum(jnp.where(onehot, starts[None, :], 0), axis=1)
        own_parent = jnp.sum(jnp.where(onehot, parents[None, :], 0), axis=1)
        parent_hot = own_parent[:, None] == seg_ids[None, :]
        parent_length = jnp.sum(jnp.where(parent_hot, lengths[None, :], 0), axis=1)
        root_depth = jnp.where(segment == 0, 0, trunk_length) + jnp.where(segment >= 5, parent_length, 0)
        token_pos = (token_index - own_start + root_depth).astype(jnp.int32)
        return (starts, parents, token_pos)
    key_list = jax.random.split(jax.random.fold_in(key, 17), TREES)
    return jax.vmap(one_tree)(key_list)


def draw_seg_start(key, part):
    return tree_layout(key)[0]


def draw_seg_parent(key, part):
    return tree_layout(key)[1]


def draw_positions(key, part):
    return tree_layout(key)[2]


def shard_levels(stream_key, dims, pieces, low, high):
    level, own = 1.0, jax.random.fold_in(stream_key, 6)
    for axis_at, parts in pieces:
        heights = jnp.exp(jax.random.uniform(jax.random.fold_in(own, axis_at), (parts,), jnp.float32, low / len(pieces), high / len(pieces)))
        level = level * jnp.repeat(heights, dims[axis_at] // parts).reshape([-1 if axis == axis_at else 1 for axis in range(len(dims))])
    return level


def noise(rng, extent, scale, bound, cuts=(), kind=jnp.bfloat16):
    factor_of = shard_levels(rng, extent, cuts, -0.22, 0.18) if cuts else 1.0
    values = jax.random.normal(rng, extent, jnp.float32) * scale * factor_of
    return jnp.minimum(jnp.maximum(values, -bound), bound).astype(kind)


def setup_inputs(seed: int = 0) -> dict:
    seeds = jax.random.split(jax.random.key(seed), 16)
    tokens = noise(seeds[0], (TREES, N_CTX, TOK_CTX, D), 1.0, 6.0, ((0, 4), (1, 4), (2, 2)))
    cotangent = noise(seeds[1], (TREES, N_CTX, TOK_CTX, D), 1.0, 6.0, ((0, 4), (1, 4), (2, 2)))
    positions = draw_positions(jax.random.fold_in(seeds[15], 71), 0)
    seg_start = draw_seg_start(jax.random.fold_in(seeds[15], 71), 0)
    seg_parent = draw_seg_parent(jax.random.fold_in(seeds[15], 71), 0)
    ln_gain = jnp.clip(1.0 + 0.1 * jax.random.normal(seeds[5], (D,), jnp.float32), 0.5, 1.5).astype(jnp.bfloat16)
    ln_bias = noise(seeds[6], (D,), 0.2, 1.25)
    w_qkv = noise(seeds[7], (D, 3, D), D ** -0.5, 0.125, ((2, 2),))
    b_qkv = noise(seeds[8], (3, D), 0.05, 0.3125, ((1, 2),))
    w_dense = noise(seeds[9], (D, D), (max(D // 256, 4)) ** -0.5, 2.0, ((0, 2),))
    b_dense = noise(seeds[10], (D,), 0.2, 1.25)
    w_fc1 = noise(seeds[11], (D, FF), D ** -0.5, 0.125, ((1, 2),))
    b_fc1 = noise(seeds[12], (FF,), 0.5, 3.0, ((0, 2),))
    w_fc2 = noise(seeds[13], (FF, D), FF ** -0.5, 0.0625, ((0, 2),))
    b_fc2 = noise(seeds[14], (D,), 0.2, 1.25)
    return {"tokens": tokens, "cotangent": cotangent, "positions": positions, "seg_start": seg_start, "seg_parent": seg_parent, "ln_gain": ln_gain, "ln_bias": ln_bias, "w_qkv": w_qkv, "b_qkv": b_qkv, "w_dense": w_dense, "b_dense": b_dense, "w_fc1": w_fc1, "b_fc1": b_fc1, "w_fc2": w_fc2, "b_fc2": b_fc2}


norm_eps = 1e-05
masked_low = -1e+30
gelu_root = 0.7978845608028654
gelu_cube = 0.044715

@jax.custom_vjp
def low(v):
    return lax.optimization_barrier(v.astype(jnp.bfloat16)).astype(jnp.float32)

@jax.custom_vjp
def low_back(v):
    return v

def low_keep(v):
    return (low(v), None)

def low_pass(kept, grad):
    return (grad,)

def back_keep(v):
    return (v, None)

def back_low(kept, grad):
    return (low(grad),)
low.defvjp(low_keep, low_pass)
low_back.defvjp(back_keep, back_low)

def gelu_tanh(values):
    return 0.5 * values * (1.0 + jnp.tanh(gelu_root * (values + gelu_cube * values * values * values)))

def segment_of(token_index, starts):
    return lax.optimization_barrier(jnp.sum((starts[None, :] <= token_index[:, None]).astype(jnp.int32), axis=1)) - 1

def parent_of(segment, parents):
    hits = segment[:, None] == jnp.arange(parents.shape[0], dtype=jnp.int32)[None, :]
    return lax.optimization_barrier(jnp.sum(jnp.where(hits, parents[None, :], 0), axis=1)).astype(jnp.int32)

def rotary_tables(token_pos):
    freq_index = jnp.arange(ROT // 2, dtype=jnp.float32)
    inverse = jnp.power(10000.0, -2.0 * freq_index / ROT)
    angles = token_pos.astype(jnp.float32)[:, None] * inverse[None, :]
    return (jnp.cos(angles), jnp.sin(angles))

def rotate(values, cosine, sine):
    half_rot = ROT // 2
    first = values[..., :half_rot]
    second = values[..., half_rot:ROT]
    cos_wide = cosine[:, None, :]
    sin_wide = sine[:, None, :]
    return jnp.concatenate([first * cos_wide - second * sin_wide, second * cos_wide + first * sin_wide, values[..., ROT:]], axis=-1)

def attention(query, key_vals, value_vals, starts, parents):
    length = query.shape[0]
    block_rows = math.gcd(length, 512)
    token_index = jnp.arange(length, dtype=jnp.int32)
    own_seg = segment_of(token_index, starts)
    up_one = parent_of(own_seg, parents)
    up_two = parent_of(up_one, parents)
    score_scale = HEAD ** (-0.5)

    def one_query_block(block_items):
        query_block, index_block, seg_block, first_up, second_up = block_items
        related = (own_seg[None, :] == seg_block[:, None]) | (own_seg[None, :] == first_up[:, None]) | (own_seg[None, :] == second_up[:, None])
        visible = (related & (token_index[None, :] <= index_block[:, None]))[:, None, :]
        scores = jnp.einsum('qhd,khd->qhk', query_block, key_vals, precision=lax.Precision.HIGHEST) * score_scale
        scores = low_back(scores)
        row_max = lax.optimization_barrier(jnp.max(jnp.where(visible, scores, masked_low), axis=2))
        weights = jnp.where(visible, jnp.exp(jnp.where(visible, scores - row_max[..., None], 0.0)), 0.0)
        row_total = lax.optimization_barrier(jnp.sum(weights, axis=2))
        summed = jnp.einsum('qhk,khd->qhd', low(weights), value_vals, precision=lax.Precision.HIGHEST)
        return summed / row_total[..., None]
    block_count = length // block_rows
    block_items = (query.reshape(block_count, block_rows, HEADS, HEAD), token_index.reshape(block_count, block_rows), own_seg.reshape(block_count, block_rows), up_one.reshape(block_count, block_rows), up_two.reshape(block_count, block_rows))
    return lax.map(jax.checkpoint(one_query_block), block_items).reshape(length, HEADS * HEAD)

def tree_forward(token_values, token_pos, starts, parents, weights_all):
    ln_gain, ln_bias, w_qkv, b_qkv, w_dense, b_dense, w_fc1, b_fc1, w_fc2, b_fc2 = weights_all
    centered = token_values - lax.optimization_barrier(jnp.mean(token_values, axis=1, keepdims=True))
    inv_std = lax.rsqrt(lax.optimization_barrier(jnp.mean(centered * centered, axis=1, keepdims=True)) + norm_eps)
    normed = low(centered * inv_std * ln_gain + ln_bias)
    qkv_pre = jnp.dot(normed, w_qkv.reshape(D, 3 * D), precision=lax.Precision.HIGHEST) + b_qkv.reshape(3 * D)
    qkv_pre = low_back(qkv_pre)
    qkv_heads = qkv_pre.reshape(-1, 3, HEADS, HEAD)
    cosine, sine = rotary_tables(token_pos)
    query = low(rotate(qkv_heads[:, 0], cosine, sine))
    key_vals = low(rotate(qkv_heads[:, 1], cosine, sine))
    value_vals = low(qkv_heads[:, 2])
    attn = low(low_back(attention(query, key_vals, value_vals, starts, parents)))
    hidden_pre = low_back(jnp.dot(normed, w_fc1, precision=lax.Precision.HIGHEST) + b_fc1)
    act_low = low(gelu_tanh(hidden_pre))
    branches = jnp.dot(attn, w_dense, precision=lax.Precision.HIGHEST) + jnp.dot(act_low, w_fc2, precision=lax.Precision.HIGHEST)
    return token_values + branches + b_dense + b_fc2

def reference(tokens, cotangent, positions, seg_start, seg_parent, ln_gain, ln_bias, w_qkv, b_qkv, w_dense, b_dense, w_fc1, b_fc1, w_fc2, b_fc2):
    weights_all = tuple((array_in.astype(jnp.float32) for array_in in (ln_gain, ln_bias, w_qkv, b_qkv, w_dense, b_dense, w_fc1, b_fc1, w_fc2, b_fc2)))

    def one_tree(running, tree_items):
        tree_tokens, tree_grad, tree_pos, tree_starts, tree_parents = tree_items
        flat_tokens = tree_tokens.reshape(TREE, D).astype(jnp.float32)

        def forward_only(token_values, *weight_list):
            return tree_forward(token_values, tree_pos, tree_starts, tree_parents, weight_list)
        result, pull_back = jax.vjp(forward_only, flat_tokens, *weights_all)
        all_grads = pull_back(tree_grad.reshape(TREE, D).astype(jnp.float32))
        running = tuple((running_sum + fresh_grad for running_sum, fresh_grad in zip(running, all_grads[1:])))
        return (running, (result.astype(jnp.bfloat16).reshape(N_CTX, TOK_CTX, D), all_grads[0].reshape(N_CTX, TOK_CTX, D)))
    start_sums = tuple((jnp.zeros_like(array_in) for array_in in weights_all))
    summed, (block_out, d_tokens) = lax.scan(one_tree, start_sums, (tokens, cotangent, positions, seg_start, seg_parent))
    return (block_out, d_tokens, summed[0], summed[1], summed[2], summed[3], summed[4], summed[5], summed[6], summed[7], summed[8], summed[9])
```

```python
import functools

import jax
import jax.numpy as jnp
from jax import lax
from jax.experimental import pallas as pl
from jax.experimental.pallas import tpu as pltpu
from jax.sharding import PartitionSpec as P

HEAD = 64
ROT = 32
LANES = 128


norm_eps = 1e-05
masked_low = -1e30
gelu_root = 0.7978845608028654
gelu_cube = 0.044715
bf16 = jnp.bfloat16
NT = (((1,), (1,)), ((), ()))
NN = (((1,), (0,)), ((), ()))
TN = (((0,), (0,)), ((), ()))


def gelu_tanh(values):
    return (
        0.5 * values * (1.0 + jnp.tanh(gelu_root * (values + gelu_cube * values * values * values)))
    )


def gelu_slope(values):
    tangent = jnp.tanh(gelu_root * (values + gelu_cube * values * values * values))
    return 0.5 * (1.0 + tangent) + 0.5 * values * (1.0 - tangent * tangent) * gelu_root * (
        1.0 + 3.0 * gelu_cube * values * values
    )


def dot32(lhs, rhs, dims):
    return lax.dot_general(lhs, rhs, dims, preferred_element_type=jnp.float32)


def rotary_tables(rows, starts, parents):
    segs = starts.shape[0]
    index = jnp.arange(rows, dtype=jnp.int32)
    place = index
    for seg in range(1, segs):
        up = parents[seg]
        depth = starts[1] + jnp.where(up == 0, 0, starts[up + 1] - starts[up])
        place = jnp.where(index >= starts[seg], index - starts[seg] + depth, place)
    freq_index = jnp.arange(ROT // 2, dtype=jnp.float32)
    inverse = jnp.power(10000.0, -2.0 * freq_index / ROT)
    angles = place.astype(jnp.float32)[:, None] * inverse[None, :]
    cosine, sine = jnp.cos(angles), jnp.sin(angles)
    half = ROT // 2
    ones = jnp.ones((rows, HEAD - ROT), jnp.float32)
    zeros = jnp.zeros((rows, half), jnp.float32)
    rest = jnp.zeros((rows, HEAD - ROT), jnp.float32)
    copies = (1, LANES // HEAD)
    return (
        jnp.tile(jnp.concatenate([cosine, cosine, ones], axis=1), copies),
        jnp.tile(jnp.concatenate([-sine, zeros, rest], axis=1), copies),
        jnp.tile(jnp.concatenate([zeros, sine, rest], axis=1), copies),
    )

def tree_attention_body(
    heads, width, tokens, q_rows, k_rows,
    starts, parents, pre_ref, grad_ref, cos_ref, low_ref, high_ref,
    attn_ref, dqkv_ref,
    key_all, val_all, key_tr, val_tr, d_key, d_val, scores, key_bits, dq_acc, out_acc,
    block_bits, chosen,
):
    step = pl.program_id(0)
    segs = starts.shape[0]
    stack = heads * q_rows
    per_key = k_rows // q_rows
    key_blocks = key_all.shape[0]
    tail_rows = tokens % q_rows
    last = pl.num_programs(0) - 1
    far = key_blocks * k_rows

    def seg_end(seg):
        return starts[seg + 1] if seg + 1 < segs else far

    def seen_bits(seg):
        up_one = parents[seg]
        up_two = parents[up_one]
        one = jnp.int32(1)
        return (
            lax.shift_left(one, jnp.int32(seg))
            | lax.shift_left(one, up_one)
            | lax.shift_left(one, up_two)
        )

    @pl.when(step == 0)
    def _():
        key_all[...] = jnp.zeros_like(key_all)
        val_all[...] = jnp.zeros_like(val_all)
        key_tr[...] = jnp.zeros_like(key_tr)
        val_tr[...] = jnp.zeros_like(val_tr)
        d_key[...] = jnp.zeros_like(d_key)
        d_val[...] = jnp.zeros_like(d_val)
        for block in range(key_blocks):
            index = block * k_rows + lax.broadcasted_iota(jnp.int32, (k_rows, q_rows), 0)
            bits = jnp.full((k_rows, q_rows), 1, jnp.int32)
            held = jnp.int32(0)
            for seg in range(segs):
                if seg:
                    bits = jnp.where(index >= starts[seg], jnp.int32(1 << seg), bits)
                inside = (starts[seg] < (block + 1) * k_rows) & (seg_end(seg) > block * k_rows)
                held = held | jnp.where(inside, jnp.int32(1 << seg), jnp.int32(0))
            key_bits[block] = bits
            block_bits[block] = held

    row_start = step * q_rows
    query_at = row_start + lax.broadcasted_iota(jnp.int32, (1, q_rows), 1)
    seen = jnp.full((1, q_rows), 1, jnp.int32)
    seen_any = jnp.int32(0)
    for seg in range(segs):
        bits = seen_bits(seg)
        if seg:
            seen = jnp.where(query_at >= starts[seg], bits, seen)
        inside = (starts[seg] < row_start + q_rows) & (seg_end(seg) > row_start)
        seen_any = seen_any | jnp.where(inside, bits, jnp.int32(0))

    def pick(block, count):
        wanted = (block_bits[block] & seen_any) != 0

        @pl.when(wanted)
        def _():
            chosen[count] = block

        return count + wanted.astype(jnp.int32)

    picked = lax.fori_loop(0, (step + per_key) // per_key, pick, jnp.int32(0))

    row_at = row_start + lax.broadcasted_iota(jnp.int32, (q_rows, LANES), 0)
    real = row_at < tokens
    cos = cos_ref[pl.ds(pl.multiple_of(row_start, q_rows), q_rows), :]
    low = low_ref[pl.ds(pl.multiple_of(row_start, q_rows), q_rows), :]
    high = high_ref[pl.ds(pl.multiple_of(row_start, q_rows), q_rows), :]

    def turn(values, sign, cos, low, high):
        return values * cos + sign * (
            pltpu.roll(values, LANES - ROT // 2, 1) * low + pltpu.roll(values, ROT // 2, 1) * high
        )

    queries, grads = [], []
    in_block = step // per_key
    in_rows = pl.ds(pl.multiple_of((step % per_key) * q_rows, q_rows), q_rows)
    for part in range(width // LANES):
        lanes = slice(part * LANES, (part + 1) * LANES)

        def piece(which):
            at = which * width + part * LANES
            return jnp.where(real, pre_ref[:, at : at + LANES], 0.0)

        queries.append(turn(piece(0), 1.0, cos, low, high).astype(jnp.bfloat16))
        key_part = turn(piece(1), 1.0, cos, low, high)
        val_part = piece(2)
        key_all[in_block, in_rows, lanes] = key_part.astype(jnp.bfloat16)
        val_all[in_block, in_rows, lanes] = val_part.astype(jnp.bfloat16)
        key_tr[step, lanes, :] = key_part.T.astype(jnp.bfloat16)
        val_tr[step, lanes, :] = val_part.T.astype(jnp.bfloat16)
        grads.append(jnp.where(real, grad_ref[:, lanes].astype(jnp.float32), 0.0))
    query = jnp.concatenate(queries, axis=1) * jnp.bfloat16(HEAD ** (-0.5))
    grad = jnp.concatenate(grads, axis=1)
    grad_tr = jnp.concatenate([part.T for part in grads], axis=0)
    lane_head = lax.broadcasted_iota(jnp.int32, (q_rows, width), 1) // HEAD
    query_stack = jnp.concatenate(
        [jnp.where(lane_head == head, query, jnp.bfloat16(0)) for head in range(heads)], axis=0
    )
    grad_low = grad.astype(jnp.bfloat16)
    grad_stack = jnp.concatenate(
        [jnp.where(lane_head == head, grad_low, jnp.bfloat16(0)) for head in range(heads)], axis=0
    )

    def transposed(cube, block):
        return jnp.concatenate([cube[block * per_key + at] for at in range(per_key)], axis=1)

    def score_block(at, row_max):
        block = chosen[at]
        raw = dot32(key_all[block], query_stack, NT)
        key_at = block * k_rows + lax.broadcasted_iota(jnp.int32, (k_rows, q_rows), 0)
        visible = ((key_bits[block] & seen) != 0) & (key_at <= query_at)
        for head in range(heads):
            lanes = slice(head * q_rows, (head + 1) * q_rows)
            scores[at, :, lanes] = jnp.where(visible, raw[:, lanes], masked_low)
        return jnp.maximum(row_max, jnp.max(scores[at], axis=0, keepdims=True))

    row_max = lax.fori_loop(
        0, picked, score_block, jnp.full((1, stack), masked_low, jnp.float32)
    )
    out_acc[...] = jnp.zeros_like(out_acc)
    dq_acc[...] = jnp.zeros_like(dq_acc)

    def weight_block(at, row_sum):
        block = chosen[at]
        weights = jnp.exp(scores[at] - row_max)
        scores[at] = weights
        out_acc[...] += dot32(transposed(val_tr, block), weights.astype(jnp.bfloat16), NN)
        return row_sum + jnp.sum(weights, axis=0, keepdims=True)

    row_sum = lax.fori_loop(0, picked, weight_block, jnp.zeros((1, stack), jnp.float32))
    inverse = 1.0 / row_sum
    outs, deltas = [], []
    for head in range(heads):
        lanes = slice(head * q_rows, (head + 1) * q_rows)
        rows = slice(head * HEAD, (head + 1) * HEAD)
        out_head = out_acc[rows, lanes] * inverse[:, lanes]
        outs.append(out_head)
        deltas.append(jnp.sum(out_head * grad_tr[rows], axis=0, keepdims=True))
    if heads * HEAD < width:
        outs.append(jnp.zeros((width - heads * HEAD, q_rows), jnp.float32))
    attn_ref[...] = jnp.concatenate(outs, axis=0).T.astype(jnp.bfloat16)
    delta = jnp.concatenate(deltas, axis=1)

    def back_block(at, unused):
        block = chosen[at]
        prob = scores[at] * inverse
        d_prob = dot32(val_all[block], grad_stack, NT)
        d_score = (prob * (d_prob - delta)).astype(jnp.bfloat16)
        dq_acc[...] += dot32(transposed(key_tr, block), d_score, NN)
        d_key[block] += dot32(d_score, query_stack, NN)
        d_val[block] += dot32(prob.astype(jnp.bfloat16), grad_stack, NN)
        return unused

    lax.fori_loop(0, picked, back_block, 0)

    def store_rows(block, which, values):
        lanes = slice(which, which + values.shape[1])

        def full():
            dqkv_ref[pl.ds(pl.multiple_of(block * q_rows, q_rows), q_rows), lanes] = values

        def short():
            dqkv_ref[tokens - tail_rows :, lanes] = values[:tail_rows]

        if not tail_rows:
            full()
        else:
            pl.when(block < last)(full)
            pl.when(block == last)(short)

    dq_heads = [
        dq_acc[head * HEAD : (head + 1) * HEAD, head * q_rows : (head + 1) * q_rows]
        for head in range(heads)
    ]
    if heads * HEAD < width:
        dq_heads.append(jnp.zeros((width - heads * HEAD, q_rows), jnp.float32))
    dq = jnp.concatenate(dq_heads, axis=0).T * (HEAD ** (-0.5))
    for part in range(width // LANES):
        turned = turn(dq[:, part * LANES : (part + 1) * LANES], -1.0, cos, low, high)
        store_rows(step, part * LANES, turned.astype(jnp.bfloat16))

    @pl.when(step == last)
    def _():
        def finish(block, unused):
            rows = pl.ds(pl.multiple_of(block * q_rows, q_rows), q_rows)
            from_rows = pl.ds(pl.multiple_of((block % per_key) * q_rows, q_rows), q_rows)
            for part in range(width // LANES):
                lanes = slice(part * LANES, (part + 1) * LANES)
                turned = turn(
                    d_key[block // per_key, from_rows, lanes],
                    -1.0, cos_ref[rows, :], low_ref[rows, :], high_ref[rows, :],
                )
                store_rows(block, width + part * LANES, turned.astype(jnp.bfloat16))
                store_rows(
                    block,
                    2 * width + part * LANES,
                    d_val[block // per_key, from_rows, lanes].astype(jnp.bfloat16),
                )
            return unused

        lax.fori_loop(0, last + 1, finish, 0)


def tree_attention(starts, parents, pre, grad, tables, heads, width, q_rows=128, k_rows=256):
    tokens = pre.shape[0]
    q_blocks = pl.cdiv(tokens, q_rows)
    per_key = k_rows // q_rows
    key_blocks = pl.cdiv(q_blocks, per_key)
    stack = heads * q_rows
    pairs = q_blocks * (q_blocks + 1) // 2 * q_rows * q_rows
    whole = lambda shape: pl.BlockSpec(shape, lambda i, *s: (0, 0))
    bf = jnp.bfloat16
    return pl.pallas_call(
        functools.partial(tree_attention_body, heads, width, tokens, q_rows, k_rows),
        out_shape=(
            jax.ShapeDtypeStruct((tokens, width), bf),
            jax.ShapeDtypeStruct((tokens, 3 * width), bf),
        ),
        grid_spec=pltpu.PrefetchScalarGridSpec(
            num_scalar_prefetch=2,
            grid=(q_blocks,),
            in_specs=[
                pl.BlockSpec((q_rows, 3 * width), lambda i, *s: (i, 0)),
                pl.BlockSpec((q_rows, width), lambda i, *s: (i, 0)),
            ]
            + [whole(tables[0].shape)] * 3,
            out_specs=[
                pl.BlockSpec((q_rows, width), lambda i, *s: (i, 0)),
                whole((tokens, 3 * width)),
            ],
            scratch_shapes=[
                pltpu.VMEM((key_blocks, k_rows, width), bf),
                pltpu.VMEM((key_blocks, k_rows, width), bf),
                pltpu.VMEM((key_blocks * per_key, width, q_rows), bf),
                pltpu.VMEM((key_blocks * per_key, width, q_rows), bf),
                pltpu.VMEM((key_blocks, k_rows, width), jnp.float32),
                pltpu.VMEM((key_blocks, k_rows, width), jnp.float32),
                pltpu.VMEM((key_blocks, k_rows, stack), jnp.float32),
                pltpu.VMEM((key_blocks, k_rows, q_rows), jnp.int32),
                pltpu.VMEM((width, stack), jnp.float32),
                pltpu.VMEM((width, stack), jnp.float32),
                pltpu.SMEM((key_blocks,), jnp.int32),
                pltpu.SMEM((key_blocks,), jnp.int32),
            ],
        ),
        compiler_params=pltpu.CompilerParams(
            dimension_semantics=("arbitrary",), vmem_limit_bytes=60 << 20
        ),
        cost_estimate=pl.CostEstimate(
            flops=12 * pairs * heads * width,
            bytes_accessed=tokens * width * 24,
            transcendentals=pairs * heads,
        ),
        name="tree_attention",
    )(starts, parents, pre, grad, *tables)


def shards(
    tokens,
    cotangent,
    positions,
    seg_start,
    seg_parent,
    ln_gain,
    ln_bias,
    w_qkv,
    b_qkv,
    w_dense,
    b_dense,
    w_fc1,
    b_fc1,
    w_fc2,
    b_fc2,
):
    own_rows, model_width = tokens.shape[2:]
    ctx = lax.axis_size("ctx")
    rep = lax.axis_size("rep")
    mine = lax.axis_index("ctx")
    tree = own_rows * ctx * lax.axis_size("tp")
    head_lanes = w_qkv.shape[2] // ctx
    heads = head_lanes // HEAD
    width = max(head_lanes, LANES)
    units = w_fc1.shape[1] // ctx
    row_split = model_width // (ctx * rep)
    starts = seg_start[0]
    parents = seg_parent[0]

    residual = tokens.reshape(own_rows, model_width).astype(jnp.float32)
    centered = residual - jnp.mean(residual, axis=1, keepdims=True)
    inv_std = lax.rsqrt(jnp.mean(centered * centered, axis=1, keepdims=True) + norm_eps)
    unit_norm = centered * inv_std
    gain_wide = ln_gain.astype(jnp.float32)
    normed_own = (unit_norm * gain_wide + ln_bias.astype(jnp.float32)).astype(bf16)
    grad_own = cotangent.reshape(own_rows, model_width)
    normed = lax.all_gather(normed_own, ("ctx", "tp"), axis=0, tiled=True)
    grad = lax.all_gather(grad_own, ("ctx", "tp"), axis=0, tiled=True)

    def own_heads(array, axis):
        part = lax.dynamic_slice_in_dim(array, mine * head_lanes, head_lanes, axis)
        if width > head_lanes:
            pads = [(0, 0)] * part.ndim
            pads[axis] = (0, width - head_lanes)
            part = jnp.pad(part, pads)
        return part

    qkv_parts = own_heads(jnp.transpose(w_qkv, (1, 0, 2)), 2)
    qkv_own = jnp.concatenate([qkv_parts[0], qkv_parts[1], qkv_parts[2]], axis=1)
    qkv_bias = own_heads(b_qkv, 1).reshape(3 * width).astype(jnp.float32)
    dense_own = own_heads(w_dense, 0)
    fc1_own = lax.dynamic_slice_in_dim(w_fc1, mine * units, units, 1)
    fc1_bias = lax.dynamic_slice_in_dim(b_fc1, mine * units, units, 0).astype(jnp.float32)
    fc2_own = lax.dynamic_slice_in_dim(w_fc2, mine * units, units, 0)

    q_rows = 128
    padded = pl.cdiv(tree, q_rows) * q_rows
    tables = rotary_tables(padded, starts, parents)

    hidden_pre = dot32(normed, fc1_own, NN) + fc1_bias
    act_low = gelu_tanh(hidden_pre).astype(bf16)
    grad_fc2 = dot32(act_low, grad, TN).astype(bf16)
    sum_fc2 = lax.psum_scatter(grad_fc2, "rep", scatter_dimension=0, tiled=True)
    d_act = dot32(grad, fc2_own, NT)
    d_hidden_low = (d_act * gelu_slope(hidden_pre)).astype(bf16)

    def by_owner(partial):
        cols = partial.shape[1]
        return (
            partial.reshape(ctx, rep, row_split, cols)
            .transpose(1, 0, 2, 3)
            .reshape(model_width, cols)
        )

    def to_rows(summed):
        return lax.all_to_all(
            summed.reshape(ctx, row_split, summed.shape[1]), "ctx", 0, 0, tiled=True
        )

    grad_fc1 = dot32(normed, d_hidden_low, TN).astype(bf16)
    sum_fc1 = to_rows(
        lax.psum_scatter(by_owner(grad_fc1), "rep", scatter_dimension=0, tiled=True)
    )
    sum_fc1 = sum_fc1.transpose(1, 0, 2).reshape(row_split, ctx * units).astype(jnp.float32)

    qkv_pre = dot32(normed, qkv_own, NN) + qkv_bias
    d_attn_low = dot32(grad, dense_own, NT).astype(bf16)
    attn_low, d_qkv_low = tree_attention(
        starts, parents, qkv_pre, d_attn_low, tables, heads, width, q_rows
    )
    branches = lax.psum_scatter(
        (dot32(attn_low, dense_own, NN) + dot32(act_low, fc2_own, NN)).astype(bf16),
        ("ctx", "tp"),
        scatter_dimension=0,
        tiled=True,
    ).astype(jnp.float32)
    block_out = (
        (residual + branches + b_dense.astype(jnp.float32) + b_fc2.astype(jnp.float32))
        .astype(bf16)
        .reshape(tokens.shape)
    )
    grad_qkv = dot32(normed, d_qkv_low, TN).astype(bf16)
    if width > head_lanes:
        grad_qkv = grad_qkv.reshape(model_width, 3, width)[:, :, :head_lanes]
        grad_qkv = grad_qkv.reshape(model_width, 3 * head_lanes)
    sum_qkv = to_rows(
        lax.psum_scatter(by_owner(grad_qkv), "rep", scatter_dimension=0, tiled=True)
    )
    sum_qkv = (
        sum_qkv.reshape(ctx, row_split, 3, head_lanes)
        .transpose(1, 2, 0, 3)
        .reshape(row_split, 3, ctx * head_lanes)
        .astype(jnp.float32)
    )
    grad_dense = dot32(attn_low, grad, TN)[:head_lanes].astype(bf16)
    sum_dense = lax.psum_scatter(grad_dense, "rep", scatter_dimension=0, tiled=True)

    d_normed = lax.psum_scatter(
        (dot32(d_qkv_low, qkv_own, NT) + dot32(d_hidden_low, fc1_own, NT)).astype(bf16),
        ("ctx", "tp"),
        scatter_dimension=0,
        tiled=True,
    ).astype(jnp.float32)
    scaled = d_normed * gain_wide
    d_tokens = grad_own.astype(jnp.float32) + inv_std * (
        scaled
        - jnp.mean(scaled, axis=1, keepdims=True)
        - unit_norm * jnp.mean(scaled * unit_norm, axis=1, keepdims=True)
    )

    qkv_bias_grad = jnp.sum(d_qkv_low.astype(jnp.float32), axis=0).reshape(3, width)
    small = jnp.concatenate(
        [
            jnp.sum(d_hidden_low.astype(jnp.float32), axis=0).reshape(rep, units // rep),
            qkv_bias_grad[:, :head_lanes]
            .reshape(3, rep, head_lanes // rep)
            .transpose(1, 0, 2)
            .reshape(rep, 3 * head_lanes // rep),
            jnp.sum(
                lax.dynamic_slice_in_dim(grad, (lax.axis_index("tp") * ctx + mine) * head_lanes, head_lanes, 1)
                .astype(jnp.float32),
                axis=0,
            ).reshape(rep, head_lanes // rep),
        ],
        axis=1,
    )
    small = jnp.sum(lax.all_to_all(small, "rep", 0, 0, tiled=True), axis=0)
    fc1_bias_grad = small[: units // rep]
    qkv_bias_grad = small[units // rep : units // rep + 3 * head_lanes // rep].reshape(3, -1)
    out_bias_grad = small[units // rep + 3 * head_lanes // rep :]

    everyone = ("tp", "ctx", "rep")
    norm_grads = jnp.stack(
        [jnp.sum(d_normed * unit_norm, axis=0), jnp.sum(d_normed, axis=0)], axis=0
    )
    norm_grads = lax.psum(norm_grads, everyone)
    place = (lax.axis_index("tp") * ctx + mine) * rep + lax.axis_index("rep")
    share = model_width // (lax.axis_size("tp") * ctx * rep)
    norm_grads = lax.dynamic_slice_in_dim(norm_grads, place * share, share, 1)
    return (
        block_out,
        d_tokens.reshape(tokens.shape),
        norm_grads[0],
        norm_grads[1],
        sum_qkv,
        qkv_bias_grad,
        sum_dense.astype(jnp.float32),
        out_bias_grad,
        sum_fc1,
        fc1_bias_grad,
        sum_fc2.astype(jnp.float32),
        out_bias_grad,
    )


def solution(mesh):
    return jax.shard_map(
        shards,
        mesh=mesh,
        in_specs=(
            P("rep", "ctx", "tp", None),
            P("rep", "ctx", "tp", None),
            P("rep", "ctx"),
            P("rep", None),
            P("rep", None),
            P(),
            P(),
            P(None, None, "tp"),
            P(None, "tp"),
            P("tp", None),
            P(),
            P(None, "tp"),
            P("tp"),
            P("tp", None),
            P(),
        ),
        out_specs=(
            P("rep", "ctx", "tp", None),
            P("rep", "ctx", "tp", None),
            P(("tp", "ctx", "rep")),
            P(("tp", "ctx", "rep")),
            P(("ctx", "rep"), None, "tp"),
            P(None, ("tp", "ctx", "rep")),
            P(("tp", "ctx", "rep"), None),
            P(("tp", "ctx", "rep")),
            P(("ctx", "rep"), "tp"),
            P(("tp", "ctx", "rep")),
            P(("tp", "ctx", "rep"), None),
            P(("tp", "ctx", "rep")),
        ),
        check_vma=False,
    )
```
